32 devices in a mesh: row: 4 (over y, x), col: 8 (over z, core).
Axes of the slice: x: 2, y: 2, z: 4, core: 2. Of those that a mesh axis runs over, the one named last changes fastest.
Arguments:
- tiles: float32 [384, 1024, 128], P('row', 'col'), may hold values from -0.1875 to 0.1875
- tile_row: int32 [384, 8], P('row', 'col'), may hold values from 0 to 511
- tile_col: int32 [384, 8], P('row', 'col'), may hold values from 0 to 255
- tile_count: int32 [4, 8], P('row', 'col'), may hold values from 24 to 96, as said below
- cost: float32 [8, 32768], P('col', 'row'), may hold values from -6 to 6
- rhs: float32 [4, 65536], P('row', 'col'), may hold values from -6 to 6
- lower: float32 [8, 32768], P('col', 'row'), may hold values from -2 to -0.3
- upper: float32 [8, 32768], P('col', 'row'), may hold values from 0.3 to 2
- primal_start: float32 [8, 32768], P('col', 'row'), may hold values from -0.3 to 0.3
- dual_start: float32 [4, 65536], P('row', 'col'), may hold values from 0 to 1
Outputs:
- primal_mean: float32 [8, 32768], P('col', 'row')
- dual_mean: float32 [4, 65536], P('row', 'col')
- primal_last: float32 [8, 32768], P('col', 'row')
- dual_last: float32 [4, 65536], P('row', 'col')
The draws below stay inside these ranges and needn't reach their ends.
Inputs may be any that keep to these rules, and one draw needn't show every extreme that they name: `tile_count`: live tiles of each device; some device holds 96.
All inputs are finite; a program needn't handle non-finite values.
Results may differ from the reference program's by a relative error of at most 0.0001.
Values sent between devices are 32-bit elements; how exact they have to be, the bound alone decides.
A program may use at most 64 MiB of HBM per device.

```python
import jax
import jax.numpy as jnp
from jax import lax

BS = 128
M = 262144
N = 262144
TILES = 96
ITERS = 6
N_ROW = 4
N_COL = 8


def draw_tile_count(key, part):
    devices_all = N_ROW * N_COL
    counts = jax.random.randint(key, (devices_all,), TILES // 4, TILES + 1)
    chosen = jax.random.randint(jax.random.fold_in(key, 7), (), 0, devices_all)
    counts = jnp.where(jnp.arange(devices_all) == chosen, TILES, counts)
    return counts.reshape(N_ROW, N_COL).astype(jnp.int32)


def plant(array, own_key, smallest, top_value):
    place = [jax.random.randint(jax.random.fold_in(own_key, axis), (), 0, length) for axis, length in enumerate(array.shape)]
    main_axis = array.shape.index(max(array.shape))
    next_to = place[:main_axis] + [(place[main_axis] + 1) % array.shape[main_axis]] + place[main_axis + 1:]
    return array.at[tuple(place)].set(smallest).at[tuple(next_to)].set(top_value)


def level_of(own_key, extent, cuts, least, largest):
    level, own = 1.0, jax.random.fold_in(own_key, 6)
    for position, shards_of in cuts:
        draws = jnp.exp(jax.random.uniform(jax.random.fold_in(own, position), (shards_of,), jnp.float32, least / len(cuts), largest / len(cuts)))
        level = level * jnp.repeat(draws, extent[position] // shards_of).reshape([-1 if axis == position else 1 for axis in range(len(extent))])
    return level


def bell_draw(rng, extent, scale, limit, cuts=(), kind=jnp.bfloat16):
    level = level_of(rng, extent, cuts, -0.22, 0.18) if cuts else 1.0
    array = jax.random.normal(rng, extent, jnp.float32) * scale * level
    return jnp.minimum(jnp.maximum(array, -limit), limit).astype(kind)


def setup_inputs(seed: int = 0) -> dict:
    arg_keys = jax.random.split(jax.random.key(seed), 11)
    return {
        "tiles": bell_draw(arg_keys[0], (N_ROW * TILES, N_COL * BS, BS), (BS * N_COL) ** -0.5, 0.1875, ((0, 4), (1, 8)), jnp.float32),
        "tile_row": plant(jax.random.randint(arg_keys[1], (N_ROW * TILES, N_COL), 0, M // (BS * N_ROW)), jax.random.fold_in(arg_keys[1], 1), 0, (M // (BS * N_ROW)) - 1).astype(jnp.int32),
        "tile_col": plant(jax.random.randint(arg_keys[2], (N_ROW * TILES, N_COL), 0, N // (BS * N_COL)), jax.random.fold_in(arg_keys[2], 1), 0, (N // (BS * N_COL)) - 1).astype(jnp.int32),
        "tile_count": draw_tile_count(jax.random.fold_in(arg_keys[10], 71), 0),
        "cost": bell_draw(arg_keys[4], (N_COL, N // N_COL), 1.0, 6.0, ((0, 8), (1, 4)), jnp.float32),
        "rhs": bell_draw(arg_keys[5], (N_ROW, M // N_ROW), 1.0, 6.0, ((0, 4), (1, 8)), jnp.float32),
        "lower": jnp.clip(-2.0 + 1.7 * jax.random.uniform(arg_keys[6], (N_COL, N // N_COL), jnp.float32) ** level_of(arg_keys[6], (N_COL, N // N_COL), ((0, 8), (1, 4)), -0.2, 0.2), -2.0, -0.3),
        "upper": jnp.clip(0.3 + 1.7 * jax.random.uniform(arg_keys[7], (N_COL, N // N_COL), jnp.float32) ** level_of(arg_keys[7], (N_COL, N // N_COL), ((0, 8), (1, 4)), -0.2, 0.2), 0.3, 2.0),
        "primal_start": jnp.clip(jax.random.uniform(arg_keys[8], (N_COL, N // N_COL), jnp.float32, -0.3, 0.3) * level_of(arg_keys[8], (N_COL, N // N_COL), ((0, 8), (1, 4)), -0.4, 0.0), -0.3, 0.3),
        "dual_start": jnp.clip(1.0 * jax.random.uniform(arg_keys[9], (N_ROW, M // N_ROW), jnp.float32) ** level_of(arg_keys[9], (N_ROW, M // N_ROW), ((0, 4), (1, 8)), -0.2, 0.2), 0.0, 1.0),
    }


exact = lax.Precision.HIGHEST
primal_step = 0.3
dual_step = 0.3


def reference(tiles, tile_row, tile_col, tile_count, cost, rhs, lower, upper, primal_start, dual_start):
    row_blocks = M // (BS * N_ROW)
    col_blocks = N // (BS * N_COL)
    blocks = tiles.reshape(N_ROW, TILES, N_COL, BS, BS)
    rows_index = tile_row.reshape(N_ROW, TILES, N_COL)
    cols_index = tile_col.reshape(N_ROW, TILES, N_COL)
    live = (jnp.arange(TILES, dtype=jnp.int32)[None, :, None] < tile_count[:, None, :]).astype(jnp.float32)
    row_hot = (rows_index[..., None] == jnp.arange(row_blocks, dtype=jnp.int32)).astype(jnp.float32) * live[..., None]
    col_hot = (cols_index[..., None] == jnp.arange(col_blocks, dtype=jnp.int32)).astype(jnp.float32)

    def forward(primal_blocks):
        def single(pieces):
            block_part, hot_rows, hot_cols = pieces
            taken = jnp.einsum('tck,ckj->tcj', hot_cols, primal_blocks, precision=exact)
            product = jnp.einsum('tcij,tcj->tci', block_part, taken, precision=exact)
            return jnp.einsum('tcr,tci->ri', hot_rows, product, precision=exact)
        return lax.map(single, (blocks, row_hot, col_hot))

    def backward(dual_blocks):
        def single(pieces):
            block_part, hot_rows, hot_cols, dual_part = pieces
            taken = jnp.einsum('tcr,ri->tci', hot_rows, dual_part, precision=exact)
            product = jnp.einsum('tcij,tci->tcj', block_part, taken, precision=exact)
            return jnp.einsum('tck,tcj->ckj', hot_cols, product, precision=exact)
        return jnp.sum(lax.map(single, (blocks, row_hot, col_hot, dual_blocks)), axis=0)

    primal = primal_start.reshape(N_COL, col_blocks, BS)
    dual = dual_start.reshape(N_ROW, row_blocks, BS)
    cost_blocks = cost.reshape(N_COL, col_blocks, BS)
    lower_blocks = lower.reshape(N_COL, col_blocks, BS)
    upper_blocks = upper.reshape(N_COL, col_blocks, BS)
    rhs_blocks = rhs.reshape(N_ROW, row_blocks, BS)
    extrapolated = primal
    primal_total = jnp.zeros_like(primal)
    dual_total = jnp.zeros_like(dual)
    for iteration in range(ITERS):
        dual = jnp.maximum(dual + dual_step * (rhs_blocks - forward(extrapolated)), 0.0)
        moved = primal - primal_step * (cost_blocks - backward(dual))
        primal_new = jnp.minimum(jnp.maximum(moved, lower_blocks), upper_blocks)
        extrapolated = 2.0 * primal_new - primal
        primal = primal_new
        primal_total = primal_total + primal
        dual_total = dual_total + dual
    shape_primal = (N_COL, N // N_COL)
    shape_dual = (N_ROW, M // N_ROW)
    return ((primal_total / ITERS).reshape(shape_primal), (dual_total / ITERS).reshape(shape_dual),
            primal.reshape(shape_primal), dual.reshape(shape_dual))
```

```python
import functools

import jax
import jax.numpy as jnp
from jax import lax
from jax.experimental import pallas as pl
from jax.experimental.pallas import tpu as pltpu
from jax.sharding import PartitionSpec as P

ITERS = 6
primal_step = 0.3
dual_step = 0.3
SUB = 8


def split_dot(hot, data):
    high = data.astype(jnp.bfloat16)
    rest = data - high.astype(jnp.float32)
    middle = rest.astype(jnp.bfloat16)
    low = (rest - middle.astype(jnp.float32)).astype(jnp.bfloat16)
    dot = functools.partial(jnp.dot, preferred_element_type=jnp.float32)
    return (dot(hot, low) + dot(hot, middle)) + dot(hot, high)


def kernel(
    n_row, n_col,
    tiles_hbm, tile_row, tile_col, tile_count, cost, rhs, lower, upper, primal_start, dual_start,
    primal_mean, dual_mean, primal_last, dual_last,
    tiles, flipped, y_init, x_init, c_init, z_all, p_all, y_hot, x_hot, y_column, x_column,
    y_state, b_state, x_state, c_state, l_state, u_state, extrapolated, y_total, x_total,
    tile_sem, z_send, z_recv, p_send, p_recv, yi_send, yi_recv, xi_send, xi_recv, ci_send, ci_recv,
):
    slots = tile_row.shape[0]
    sy = rhs.shape[0]
    sx = cost.shape[0]
    row = lax.axis_index("row")
    col = lax.axis_index("col")
    chips = n_col // 2
    chip = col // 2
    core = col % 2
    partner = chip * 2 + (1 - core)

    def chip_to(d):
        return ((chip + d) % chips) * 2 + core

    def chip_from(d):
        return ((chip + chips - d) % chips) * 2 + core

    def row_to(d):
        return (row + d) % n_row

    def row_from(d):
        return (row + n_row - d) % n_row

    tile_copy = pltpu.make_async_copy(tiles_hbm, tiles, tile_sem)
    tile_copy.start()

    barrier = pltpu.get_barrier_semaphore()
    for d in range(1, n_row):
        pl.semaphore_signal(barrier, inc=1, device_id={"row": row_to(d)}, device_id_type=pl.DeviceIdType.MESH)
    for d in range(1, chips):
        pl.semaphore_signal(barrier, inc=1, device_id={"col": chip_to(d)}, device_id_type=pl.DeviceIdType.MESH)
    pl.semaphore_signal(barrier, inc=1, device_id={"col": partner}, device_id_type=pl.DeviceIdType.MESH)

    live = lax.broadcasted_iota(jnp.int32, (slots, 1), 0) < tile_count[...]
    row_ids = tile_row[...].astype(jnp.float32)
    col_ids = tile_col[...].astype(jnp.float32)

    def as_row(ids):
        wide = jnp.broadcast_to(jnp.where(live, ids, -1.0), (slots, 128))
        if slots < 128:
            wide = jnp.concatenate([wide, jnp.full((128 - slots, 128), -1.0, jnp.float32)], axis=0)
        return wide.T[:SUB, :]

    x_init[row, 0:sx, :] = primal_start[...]
    x_init[row, sx : sx + SUB, :] = as_row(col_ids)
    y_init[col, 0:sy, :] = dual_start[...]
    y_init[col, sy : 2 * sy, :] = rhs[...]
    y_init[col, 2 * sy : 2 * sy + SUB, :] = as_row(row_ids)
    c_init[row, 0:sx, :] = cost[...]
    c_init[row, sx : 2 * sx, :] = lower[...]
    c_init[row, 2 * sx : 3 * sx, :] = upper[...]

    pl.semaphore_wait(barrier, (n_row - 1) + (chips - 1) + 1)

    def remote(place, send, recv, target):
        return pltpu.make_async_remote_copy(
            src_ref=place, dst_ref=place, send_sem=send, recv_sem=recv,
            device_id=target, device_id_type=pl.DeviceIdType.MESH,
        )

    def row_send(place_of, send, recv):
        for d in range(1, n_row):
            remote(place_of(row), send(d - 1), recv(d - 1), {"row": row_to(d)}).start()

    def row_wait(place_of, send, recv):
        for d in range(1, n_row):
            remote(place_of(row_from(d)), send(d - 1), recv(d - 1), {"row": row_to(d)}).wait_recv()
        for d in range(1, n_row):
            remote(place_of(row), send(d - 1), recv(d - 1), {"row": row_to(d)}).wait_send()

    near_first = sorted(range(1, chips), key=lambda d: min(d, chips - d))

    def col_send(place_of, send, recv):
        for d in near_first:
            remote(place_of(col), send(d - 1), recv(d - 1), {"col": chip_to(d)}).start()
        remote(place_of(col), send(chips - 1), recv(chips - 1), {"col": partner}).start()

    def other(index):
        return index + 1 - 2 * core

    def col_wait(place_of, send, recv):
        for d in near_first:
            remote(place_of(chip_from(d)), send(d - 1), recv(d - 1), {"col": chip_to(d)}).wait_recv()
            remote(place_of(chip_from(d)), send(chips + d - 1), recv(chips + d - 1), {"col": partner}).start()
        remote(place_of(partner), send(chips - 1), recv(chips - 1), {"col": partner}).wait_recv()
        for d in near_first:
            remote(
                place_of(other(chip_from(d))), send(chips + d - 1), recv(chips + d - 1), {"col": partner}
            ).wait_recv()
        for d in near_first:
            remote(place_of(col), send(d - 1), recv(d - 1), {"col": chip_to(d)}).wait_send()
            remote(place_of(chip_from(d)), send(chips + d - 1), recv(chips + d - 1), {"col": partner}).wait_send()
        remote(place_of(col), send(chips - 1), recv(chips - 1), {"col": partner}).wait_send()

    xi = (lambda i: x_init.at[i], lambda k: xi_send.at[k], lambda k: xi_recv.at[k])
    ci = (lambda i: c_init.at[i], lambda k: ci_send.at[k], lambda k: ci_recv.at[k])
    yi = (lambda i: y_init.at[i], lambda k: yi_send.at[k], lambda k: yi_recv.at[k])
    row_send(*xi)
    col_send(*yi)
    row_send(*ci)

    tile_copy.wait()

    def flip(t, carry):
        flipped[t] = tiles[t].T
        return carry

    lax.fori_loop(0, slots, flip, 0, unroll=4)

    def hot_of(ids, first, share, column, hot, init, at, n):
        for i in range(n):
            block = init[i, at : at + SUB, :].T
            column[i * slots : (i + 1) * slots, :] = jnp.broadcast_to(block[:slots, 0:1], (slots, 128))
        wide = column[...].T[0:1, :]
        own = first + lax.broadcasted_iota(jnp.int32, (share, 1), 0)
        hot[0:slots, :] = jnp.where(ids == wide, 1.0, 0.0).astype(jnp.bfloat16)
        hot[slots : slots + share, :] = jnp.where(own.astype(jnp.float32) == wide, 1.0, 0.0).astype(jnp.bfloat16)

    def pick_of(ids, blocks):
        return jnp.where(
            ids == lax.broadcasted_iota(jnp.int32, (slots, blocks), 1), 1.0, 0.0
        ).astype(jnp.bfloat16)

    def place_state(state, pick, init, at, share, own, n):
        whole = init[:, at : at + share, :].reshape(n * share, 128)
        state[0:slots, :] = split_dot(pick, whole)
        state[slots : slots + share, :] = own[...]

    row_wait(*xi)
    x_pick = pick_of(tile_col[...], n_row * sx)
    place_state(x_state, x_pick, x_init, 0, sx, primal_start, n_row)
    extrapolated[...] = x_state[0:slots, :]
    hot_of(col_ids, row * sx, sx, x_column, x_hot, x_init, sx, n_row)

    col_wait(*yi)
    y_pick = pick_of(tile_row[...], n_col * sy)
    place_state(y_state, y_pick, y_init, 0, sy, dual_start, n_col)
    place_state(b_state, y_pick, y_init, sy, sy, rhs, n_col)
    hot_of(row_ids, col * sy, sy, y_column, y_hot, y_init, 2 * sy, n_col)

    row_wait(*ci)
    place_state(c_state, x_pick, c_init, 0, sx, cost, n_row)
    place_state(l_state, x_pick, c_init, sx, sx, lower, n_row)
    place_state(u_state, x_pick, c_init, 2 * sx, sx, upper, n_row)

    y_total[...] = jnp.zeros_like(y_total)
    x_total[...] = jnp.zeros_like(x_total)

    def products(blocks, vectors, out):
        def group(g, carry):
            at = pl.multiple_of(g * SUB, SUB)
            columns = vectors[pl.ds(at, SUB), :].T
            rows = [
                jnp.sum(blocks[at + k] * columns[:, k : k + 1], axis=0, keepdims=True) for k in range(SUB)
            ]
            out[pl.ds(at, SUB), :] = jnp.concatenate(rows, axis=0)
            return carry

        lax.fori_loop(0, slots // SUB, group, 0, unroll=2)

    def iteration(step, carry):
        now = step % 2
        z = (lambda i: z_all.at[now, i], lambda k: z_send.at[now, k], lambda k: z_recv.at[now, k])
        p = (lambda i: p_all.at[now, i], lambda k: p_send.at[now, k], lambda k: p_recv.at[now, k])
        products(flipped, extrapolated, z_all.at[now, col])
        col_send(*z)
        col_wait(*z)
        applied = split_dot(y_hot[...], z_all[now].reshape(n_col * slots, 128))
        y_new = jnp.maximum(y_state[...] + dual_step * (b_state[...] - applied), 0.0)
        y_state[...] = y_new
        y_total[...] += y_new[slots:, :]
        products(tiles, y_state, p_all.at[now, row])
        row_send(*p)
        row_wait(*p)
        transposed = split_dot(x_hot[...], p_all[now].reshape(n_row * slots, 128))
        x_old = x_state[...]
        moved = x_old - primal_step * (c_state[...] - transposed)
        x_new = jnp.minimum(jnp.maximum(moved, l_state[...]), u_state[...])
        x_state[...] = x_new
        extrapolated[...] = 2.0 * x_new[:slots, :] - x_old[:slots, :]
        x_total[...] += x_new[slots:, :]
        return carry

    lax.fori_loop(0, ITERS, iteration, 0)

    primal_last[...] = x_state[slots:, :]
    dual_last[...] = y_state[slots:, :]
    primal_mean[...] = x_total[...] / ITERS
    dual_mean[...] = y_total[...] / ITERS


def body(n_row, n_col, tiles, tile_row, tile_col, tile_count, cost, rhs, lower, upper, primal_start, dual_start):
    slots, bs = tiles.shape[0], tiles.shape[2]
    blocks = [a.reshape(-1, bs) for a in (cost, rhs, lower, upper, primal_start, dual_start)]
    sx, sy = blocks[0].shape[0], blocks[1].shape[0]
    f32 = jnp.float32
    chips = n_col // 2
    vmem = pl.BlockSpec(memory_space=pltpu.VMEM)
    dma = pltpu.SemaphoreType.DMA
    state = lambda share: pltpu.VMEM((slots + share, bs), f32)
    out = pl.pallas_call(
        functools.partial(kernel, n_row, n_col),
        out_shape=[jax.ShapeDtypeStruct((s, bs), f32) for s in (sx, sy, sx, sy)],
        in_specs=[pl.BlockSpec(memory_space=pl.ANY)] + [vmem] * 9,
        out_specs=[vmem] * 4,
        scratch_shapes=[
            pltpu.VMEM(tiles.shape, f32),
            pltpu.VMEM(tiles.shape, f32),
            pltpu.VMEM((n_col, 2 * sy + SUB, bs), f32),
            pltpu.VMEM((n_row, sx + SUB, bs), f32),
            pltpu.VMEM((n_row, 3 * sx, bs), f32),
            pltpu.VMEM((2, n_col, slots, bs), f32),
            pltpu.VMEM((2, n_row, slots, bs), f32),
            pltpu.VMEM((slots + sy, n_col * slots), jnp.bfloat16),
            pltpu.VMEM((slots + sx, n_row * slots), jnp.bfloat16),
            pltpu.VMEM((n_col * slots, bs), f32),
            pltpu.VMEM((n_row * slots, bs), f32),
            state(sy), state(sy), state(sx), state(sx), state(sx), state(sx),
            pltpu.VMEM((slots, bs), f32),
            pltpu.VMEM((sy, bs), f32),
            pltpu.VMEM((sx, bs), f32),
            dma,
            dma((2, 2 * chips)), dma((2, 2 * chips)),
            dma((2, n_row)), dma((2, n_row)),
            dma((2 * chips,)), dma((2 * chips,)),
            dma((n_row,)), dma((n_row,)),
            dma((n_row,)), dma((n_row,)),
        ],
        compiler_params=pltpu.CompilerParams(
            collective_id=0, has_side_effects=True, vmem_limit_bytes=40 * 1024 * 1024
        ),
        name="pdhg",
    )(tiles, tile_row, tile_col, tile_count, *blocks)
    return tuple(a.reshape(1, -1) for a in out)


def solution(mesh):
    return jax.shard_map(
        functools.partial(body, mesh.shape["row"], mesh.shape["col"]),
        mesh=mesh,
        in_specs=(
            P("row", "col", None),
            P("row", "col"),
            P("row", "col"),
            P("row", "col"),
            P("col", "row"),
            P("row", "col"),
            P("col", "row"),
            P("col", "row"),
            P("col", "row"),
            P("row", "col"),
        ),
        out_specs=(P("col", "row"), P("row", "col"), P("col", "row"), P("row", "col")),
        check_vma=False,
    )
```

```python
import functools

import jax
import jax.numpy as jnp
from jax import lax
from jax.experimental import pallas as pl
from jax.experimental.pallas import tpu as pltpu
from jax.sharding import PartitionSpec as P

ITERS = 6
primal_step = 0.3
dual_step = 0.3
SUB = 8
CHUNKS = 2
TILE_PARTS = 4
UNROLL = 6


def split_dot(hot, data):
    high = data.astype(jnp.bfloat16)
    rest = data - high.astype(jnp.float32)
    middle = rest.astype(jnp.bfloat16)
    low = (rest - middle.astype(jnp.float32)).astype(jnp.bfloat16)
    dot = functools.partial(jnp.dot, preferred_element_type=jnp.float32)
    return (dot(hot, low) + dot(hot, middle)) + dot(hot, high)


def pieces_of(data):
    high = data.astype(jnp.bfloat16).astype(jnp.float32)
    rest = data - high
    middle = rest.astype(jnp.bfloat16).astype(jnp.float32)
    return high, middle, rest - middle


def kernel(
    n_row, n_col,
    tiles_hbm, tile_row, tile_col, tile_count, cost, rhs, lower, upper, primal_start, dual_start,
    primal_mean, dual_mean, primal_last, dual_last,
    tiles, plain, flipped, y_init, x_init, c_init, z_all, p_all, y_hot, x_hot, y_column, x_column,
    y_state, b_state, x_state, c_state, l_state, u_state, extrapolated, y_total, x_total,
    tile_sem, in_sem, z_send, z_recv, p_send, p_recv, yi_send, yi_recv, xi_send, xi_recv, ci_send, ci_recv,
):
    slots = tile_row.shape[1]
    sy = rhs.shape[0]
    sx = cost.shape[0]
    row = lax.axis_index("row")
    col = lax.axis_index("col")
    chips = n_col // 2
    chip = col // 2
    core = col % 2
    partner = chip * 2 + (1 - core)
    high_half = (chip * 2) // chips

    def chip_at(k):
        down = chips - 1 - k
        down = down - (chip - down + chips) // chips
        up = k + (k - chip + chips) // chips
        return (1 - high_half) * down + high_half * up

    def row_to(d):
        return (row + d) % n_row

    def row_from(d):
        return (row + n_row - d) % n_row

    local = [
        pltpu.make_async_copy(source, place, in_sem.at[i])
        for i, (source, place) in enumerate(
            [
                (primal_start, x_init.at[row, 0:sx]),
                (dual_start, y_init.at[col, 0:sy]),
                (rhs, y_init.at[col, sy : 2 * sy]),
                (cost, c_init.at[row, 0:sx]),
                (lower, c_init.at[row, sx : 2 * sx]),
                (upper, c_init.at[row, 2 * sx : 3 * sx]),
            ]
        )
    ]
    for copy in local:
        copy.start()
    part = slots // TILE_PARTS
    tile_copies = [
        pltpu.make_async_copy(
            tiles_hbm.at[i * part : (i + 1) * part], tiles.at[i * part : (i + 1) * part], tile_sem.at[i]
        )
        for i in range(TILE_PARTS)
    ]
    for copy in tile_copies:
        copy.start()

    mesh_id = pl.DeviceIdType.MESH
    barrier = pltpu.get_barrier_semaphore()
    for d in range(1, n_row):
        pl.semaphore_signal(barrier, inc=1, device_id={"row": row_to(d)}, device_id_type=mesh_id)
    for k in range(chips - 1):
        pl.semaphore_signal(
            barrier, inc=1, device_id={"col": chip_at(k) * 2 + core}, device_id_type=mesh_id
        )
    pl.semaphore_signal(barrier, inc=1, device_id={"col": partner}, device_id_type=mesh_id)

    live = lax.broadcasted_iota(jnp.int32, (1, slots), 1) < tile_count[...]
    for ids, init, me, at in ((tile_row, y_init, col, 2 * sy), (tile_col, x_init, row, sx)):
        init[me, at : at + SUB, :] = jnp.full((SUB, 128), -1.0, jnp.float32)
        init[me, at : at + SUB, 0:slots] = jnp.broadcast_to(
            jnp.where(live, ids[...].astype(jnp.float32), -1.0), (SUB, slots)
        )

    def remote(place, send, recv, target):
        return pltpu.make_async_remote_copy(
            src_ref=place, dst_ref=place, send_sem=send, recv_sem=recv, device_id=target, device_id_type=mesh_id
        )

    def row_send(place_of, send, recv, c):
        for d in range(1, n_row):
            remote(place_of(row, c), send(d - 1, c), recv(d - 1, c), {"row": row_to(d)}).start()

    def row_wait(place_of, send, recv, chunks):
        for c in range(chunks):
            for d in range(1, n_row):
                remote(place_of(row_from(d), c), send(d - 1, c), recv(d - 1, c), {"row": row_to(d)}).wait_recv()
        for c in range(chunks):
            for d in range(1, n_row):
                remote(place_of(row, c), send(d - 1, c), recv(d - 1, c), {"row": row_to(d)}).wait_send()

    def col_send(place_of, send, recv, c):
        for k in range(chips - 1):
            there = chip_at(k)
            remote(place_of(col, c), send(there, c), recv(chip, c), {"col": there * 2 + core}).start()
        remote(place_of(col, c), send(chip, c), recv(chip, c), {"col": partner}).start()

    def col_wait(place_of, send, recv, chunks):
        order = [(c, k) for c in range(chunks) for k in reversed(range(chips - 1))]
        to_partner = {"col": partner}
        for c, k in order:
            there = chip_at(k)
            block = place_of(there * 2 + core, c)
            remote(block, send(there, c), recv(there, c), to_partner).wait_recv()
            remote(block, send(chips + there, c), recv(chips + there, c), to_partner).start()
        for c in range(chunks):
            remote(place_of(partner, c), send(chip, c), recv(chip, c), to_partner).wait_recv()
        for c, k in order:
            there = chip_at(k)
            block = place_of(there * 2 + 1 - core, c)
            remote(block, send(chips + there, c), recv(chips + there, c), to_partner).wait_recv()
        for c, k in order:
            there = chip_at(k)
            remote(place_of(col, c), send(there, c), recv(chip, c), to_partner).wait_send()
            block = place_of(there * 2 + core, c)
            remote(block, send(chips + there, c), recv(chips + there, c), to_partner).wait_send()
        for c in range(chunks):
            remote(place_of(col, c), send(chip, c), recv(chip, c), to_partner).wait_send()

    def whole(buffer, send, recv):
        return (lambda i, c: buffer.at[i], lambda k, c: send.at[k], lambda k, c: recv.at[k])

    def sliced(buffer, send, recv, now):
        size = slots // CHUNKS
        return (
            lambda i, c: buffer.at[now, i, c * size : (c + 1) * size],
            lambda k, c: send.at[now, k, c],
            lambda k, c: recv.at[now, k, c],
        )

    xi = whole(x_init, xi_send, xi_recv)
    ci = whole(c_init, ci_send, ci_recv)
    yi = whole(y_init, yi_send, yi_recv)
    local[0].wait()
    pl.semaphore_wait(barrier, (n_row - 1) + (chips - 1) + 1)
    row_send(*xi, 0)
    for copy in local[1:3]:
        copy.wait()
    col_send(*yi, 0)
    for copy in local[3:]:
        copy.wait()
    row_send(*ci, 0)

    def pair_up(q, carry):
        for half in range(2):
            tile = tiles[2 * q + half]
            for out, data in ((plain, tile), (flipped, tile.T)):
                high = data.astype(jnp.bfloat16)
                out[q, 0:128, half * 128 : half * 128 + 128] = high
                out[q, 128:256, half * 128 : half * 128 + 128] = (
                    data - high.astype(jnp.float32)
                ).astype(jnp.bfloat16)
        return carry

    for i in range(TILE_PARTS):
        tile_copies[i].wait()
        lax.fori_loop(i * part // 2, (i + 1) * part // 2, pair_up, 0, unroll=2)

    def column_of(init, i, at):
        return init[i, at : at + SUB, :].T[:slots, 0:1]

    def own_ids(init, me, at):
        ids = column_of(init, me, at)
        return jnp.where(ids < 0.0, -2.0, ids)

    def hot_of(ids, first, share, column, hot, init, at, n):
        for i in range(n):
            column[i * slots : (i + 1) * slots, :] = jnp.broadcast_to(column_of(init, i, at), (slots, 128))
        wide = column[...].T[0:1, :]
        own = first + lax.broadcasted_iota(jnp.int32, (share, 1), 0)
        hot[0:slots, :] = jnp.where(ids == wide, 1.0, 0.0).astype(jnp.bfloat16)
        hot[slots : slots + share, :] = jnp.where(own.astype(jnp.float32) == wide, 1.0, 0.0).astype(jnp.bfloat16)

    def pick_of(ids, blocks):
        lanes = lax.broadcasted_iota(jnp.int32, (slots, blocks), 1).astype(jnp.float32)
        return jnp.where(ids == lanes, 1.0, 0.0).astype(jnp.bfloat16)

    def place_state(state, pick, init, at, share, me, n):
        state[0:slots, :] = split_dot(pick, init[:, at : at + share, :].reshape(n * share, 128))
        state[slots : slots + share, :] = init[me, at : at + share, :]

    def products(pairs, vectors, out, send):
        line = lax.broadcasted_iota(jnp.int32, (SUB, 128), 0)
        per_chunk = slots // SUB // CHUNKS

        def group(g, carry):
            at = pl.multiple_of(g * SUB, SUB)
            left = jnp.concatenate(pieces_of(vectors[pl.ds(at, SUB), :]), axis=0).astype(jnp.bfloat16)
            left = jnp.concatenate([left, left], axis=1)
            result = jnp.zeros((SUB, 128), jnp.float32)
            for q in range(SUB // 2):
                both = jnp.dot(left, pairs[g * (SUB // 2) + q], preferred_element_type=jnp.float32)
                total = (both[2 * SUB :] + both[SUB : 2 * SUB]) + both[:SUB]
                result = jnp.where(line == 2 * q, total[:, :128], result)
                result = jnp.where(line == 2 * q + 1, total[:, 128:], result)
            out[pl.ds(at, SUB), :] = result
            return carry

        for c in range(CHUNKS):
            lax.fori_loop(c * per_chunk, (c + 1) * per_chunk, group, 0, unroll=UNROLL)
            send(c)

    def forward(now):
        z = sliced(z_all, z_send, z_recv, now)
        products(flipped, extrapolated, z_all.at[now, col], lambda c: col_send(*z, c))

    row_wait(*xi, 1)
    col_ids = own_ids(x_init, row, sx)
    x_pick = pick_of(col_ids, n_row * sx)
    place_state(x_state, x_pick, x_init, 0, sx, row, n_row)
    extrapolated[...] = x_state[0:slots, :]
    forward(0)

    hot_of(col_ids, row * sx, sx, x_column, x_hot, x_init, sx, n_row)
    row_wait(*ci, 1)
    place_state(c_state, x_pick, c_init, 0, sx, row, n_row)
    place_state(l_state, x_pick, c_init, sx, sx, row, n_row)
    place_state(u_state, x_pick, c_init, 2 * sx, sx, row, n_row)
    col_wait(*yi, 1)
    row_ids = own_ids(y_init, col, 2 * sy)
    y_pick = pick_of(row_ids, n_col * sy)
    place_state(y_state, y_pick, y_init, 0, sy, col, n_col)
    place_state(b_state, y_pick, y_init, sy, sy, col, n_col)
    hot_of(row_ids, col * sy, sy, y_column, y_hot, y_init, 2 * sy, n_col)
    y_total[...] = jnp.zeros_like(y_total)
    x_total[...] = jnp.zeros_like(x_total)

    def iteration(step, carry):
        now = step % 2
        z = sliced(z_all, z_send, z_recv, now)
        p = sliced(p_all, p_send, p_recv, now)
        col_wait(*z, CHUNKS)
        applied = split_dot(y_hot[...], z_all[now].reshape(n_col * slots, 128))
        y_new = jnp.maximum(y_state[...] + dual_step * (b_state[...] - applied), 0.0)
        y_state[...] = y_new
        products(plain, y_state, p_all.at[now, row], lambda c: row_send(*p, c))
        y_total[...] += y_new[slots:, :]
        row_wait(*p, CHUNKS)
        transposed = split_dot(x_hot[...], p_all[now].reshape(n_row * slots, 128))
        x_old = x_state[...]
        moved = x_old - primal_step * (c_state[...] - transposed)
        x_new = jnp.minimum(jnp.maximum(moved, l_state[...]), u_state[...])
        x_state[...] = x_new
        extrapolated[...] = 2.0 * x_new[:slots, :] - x_old[:slots, :]

        @pl.when(step < ITERS - 1)
        def _():
            forward(1 - now)

        x_total[...] += x_new[slots:, :]
        return carry

    lax.fori_loop(0, ITERS, iteration, 0)

    primal_last[...] = x_state[slots:, :]
    dual_last[...] = y_state[slots:, :]
    primal_mean[...] = x_total[...] / ITERS
    dual_mean[...] = y_total[...] / ITERS


def body(n_row, n_col, tiles, tile_row, tile_col, tile_count, cost, rhs, lower, upper, primal_start, dual_start):
    slots, bs = tiles.shape[0], tiles.shape[2]
    blocks = [a.reshape(-1, bs) for a in (cost, rhs, lower, upper, primal_start, dual_start)]
    sx, sy = blocks[0].shape[0], blocks[1].shape[0]
    f32 = jnp.float32
    chips = n_col // 2
    vmem = pl.BlockSpec(memory_space=pltpu.VMEM)
    hbm = pl.BlockSpec(memory_space=pltpu.HBM)
    dma = pltpu.SemaphoreType.DMA
    state = lambda share: pltpu.VMEM((slots + share, bs), f32)
    out = pl.pallas_call(
        functools.partial(kernel, n_row, n_col),
        out_shape=[jax.ShapeDtypeStruct((s, bs), f32) for s in (sx, sy, sx, sy)],
        in_specs=[hbm] + [vmem] * 3 + [hbm] * 6,
        out_specs=[vmem] * 4,
        scratch_shapes=[
            pltpu.VMEM(tiles.shape, f32),
            pltpu.VMEM((slots // 2, 2 * bs, 2 * bs), jnp.bfloat16),
            pltpu.VMEM((slots // 2, 2 * bs, 2 * bs), jnp.bfloat16),
            pltpu.VMEM((n_col, 2 * sy + SUB, bs), f32),
            pltpu.VMEM((n_row, sx + SUB, bs), f32),
            pltpu.VMEM((n_row, 3 * sx, bs), f32),
            pltpu.VMEM((2, n_col, slots, bs), f32),
            pltpu.VMEM((2, n_row, slots, bs), f32),
            pltpu.VMEM((slots + sy, n_col * slots), jnp.bfloat16),
            pltpu.VMEM((slots + sx, n_row * slots), jnp.bfloat16),
            pltpu.VMEM((n_col * slots, bs), f32),
            pltpu.VMEM((n_row * slots, bs), f32),
            state(sy), state(sy), state(sx), state(sx), state(sx), state(sx),
            pltpu.VMEM((slots, bs), f32),
            pltpu.VMEM((sy, bs), f32),
            pltpu.VMEM((sx, bs), f32),
            dma((TILE_PARTS,)), dma((6,)),
            dma((2, 2 * chips, CHUNKS)), dma((2, 2 * chips, CHUNKS)),
            dma((2, n_row, CHUNKS)), dma((2, n_row, CHUNKS)),
            dma((2 * chips,)), dma((2 * chips,)),
            dma((n_row,)), dma((n_row,)),
            dma((n_row,)), dma((n_row,)),
        ],
        compiler_params=pltpu.CompilerParams(
            collective_id=0, has_side_effects=True, vmem_limit_bytes=40 * 1024 * 1024
        ),
        name="pdhg",
    )(tiles, tile_row.reshape(1, slots), tile_col.reshape(1, slots), tile_count, *blocks)
    return tuple(a.reshape(1, -1) for a in out)


def solution(mesh):
    return jax.shard_map(
        functools.partial(body, mesh.shape["row"], mesh.shape["col"]),
        mesh=mesh,
        in_specs=(
            P("row", "col", None),
            P("row", "col"),
            P("row", "col"),
            P("row", "col"),
            P("col", "row"),
            P("row", "col"),
            P("col", "row"),
            P("col", "row"),
            P("col", "row"),
            P("row", "col"),
        ),
        out_specs=(P("col", "row"), P("row", "col"), P("col", "row"), P("row", "col")),
        check_vma=False,
    )
```

```python
import functools

import jax
import jax.numpy as jnp
from jax import lax
from jax.experimental import pallas as pl
from jax.experimental.pallas import tpu as pltpu
from jax.sharding import PartitionSpec as P

ITERS = 6
primal_step = 0.3
dual_step = 0.3
SUB = 8
CHUNKS = 3
TILE_PARTS = 4
UNROLL = 4
VMEM_BYTES = 62 * 1024 * 1024


def split_dot(hot, data):
    high = data.astype(jnp.bfloat16)
    rest = data - high.astype(jnp.float32)
    middle = rest.astype(jnp.bfloat16)
    low = (rest - middle.astype(jnp.float32)).astype(jnp.bfloat16)
    dot = functools.partial(jnp.dot, preferred_element_type=jnp.float32)
    return (dot(hot, low) + dot(hot, middle)) + dot(hot, high)


def pieces_of(data):
    high = data.astype(jnp.bfloat16).astype(jnp.float32)
    rest = data - high
    middle = rest.astype(jnp.bfloat16).astype(jnp.float32)
    return high, middle, rest - middle


def kernel(
    n_row, n_col,
    tiles_hbm, tile_row, tile_col, tile_count, cost, rhs, lower, upper, primal_start, dual_start,
    primal_mean, dual_mean, primal_last, dual_last,
    tiles, plain, flipped, y_init, x_init, c_init, z_all, p_all, y_hot, x_hot, y_column, x_column,
    y_state, b_state, x_state, c_state, l_state, u_state, extrapolated, y_total, x_total,
    row_line, col_line, count_cell, tile_sem, in_sem, z_send, z_recv, p_send, p_recv, yi_send, yi_recv, xi_send, xi_recv, ci_send, ci_recv,
):
    slots = tile_row.shape[1]
    sy = rhs.shape[0]
    sx = cost.shape[0]
    row = lax.axis_index("row")
    col = lax.axis_index("col")
    chips = n_col // 2
    chip = col // 2
    core = col % 2
    partner = chip * 2 + (1 - core)
    high_half = (chip * 2) // chips

    def chip_at(k):
        down = chips - 1 - k
        down = down - (chip - down + chips) // chips
        up = k + (k - chip + chips) // chips
        return (1 - high_half) * down + high_half * up

    def row_to(d):
        return (row + d) % n_row

    def row_from(d):
        return (row + n_row - d) % n_row

    local = [
        pltpu.make_async_copy(source, place, in_sem.at[i])
        for i, (source, place) in enumerate(
            [
                (primal_start, x_init.at[row, 0:sx]),
                (dual_start, y_init.at[col, 0:sy]),
                (rhs, y_init.at[col, sy : 2 * sy]),
                (cost, c_init.at[row, 0:sx]),
                (lower, c_init.at[row, sx : 2 * sx]),
                (upper, c_init.at[row, 2 * sx : 3 * sx]),
                (tile_row, row_line),
                (tile_col, col_line),
                (tile_count, count_cell),
            ]
        )
    ]
    for copy in local:
        copy.start()
    part = slots // TILE_PARTS
    tile_copies = [
        pltpu.make_async_copy(
            tiles_hbm.at[i * part : (i + 1) * part], tiles.at[i * part : (i + 1) * part], tile_sem.at[i]
        )
        for i in range(TILE_PARTS)
    ]
    for copy in tile_copies:
        copy.start()

    mesh_id = pl.DeviceIdType.MESH
    barrier = pltpu.get_barrier_semaphore()
    for d in range(1, n_row):
        pl.semaphore_signal(barrier, inc=1, device_id={"row": row_to(d)}, device_id_type=mesh_id)
    for k in range(chips - 1):
        pl.semaphore_signal(
            barrier, inc=1, device_id={"col": chip_at(k) * 2 + core}, device_id_type=mesh_id
        )
    pl.semaphore_signal(barrier, inc=1, device_id={"col": partner}, device_id_type=mesh_id)

    for copy in local[6:]:
        copy.wait()
    live = lax.broadcasted_iota(jnp.int32, (1, slots), 1) < count_cell[...]
    for ids, init, me, at in ((row_line, y_init, col, 2 * sy), (col_line, x_init, row, sx)):
        init[me, at : at + SUB, :] = jnp.full((SUB, 128), -1.0, jnp.float32)
        init[me, at : at + SUB, 0:slots] = jnp.broadcast_to(
            jnp.where(live, ids[...].astype(jnp.float32), -1.0), (SUB, slots)
        )

    def remote(place, send, recv, target):
        return pltpu.make_async_remote_copy(
            src_ref=place, dst_ref=place, send_sem=send, recv_sem=recv, device_id=target, device_id_type=mesh_id
        )

    def row_send(place_of, send, recv, c):
        for d in range(1, n_row):
            remote(place_of(row, c), send(d - 1, c), recv(d - 1, c), {"row": row_to(d)}).start()

    def row_wait(place_of, send, recv, chunks):
        for c in range(chunks):
            for d in range(1, n_row):
                remote(place_of(row_from(d), c), send(d - 1, c), recv(d - 1, c), {"row": row_to(d)}).wait_recv()
        for c in range(chunks):
            for d in range(1, n_row):
                remote(place_of(row, c), send(d - 1, c), recv(d - 1, c), {"row": row_to(d)}).wait_send()

    def col_send(place_of, send, recv, c):
        for k in range(chips - 1):
            there = chip_at(k)
            remote(place_of(col, c), send(there, c), recv(chip, c), {"col": there * 2 + core}).start()
        remote(place_of(col, c), send(chip, c), recv(chip, c), {"col": partner}).start()

    def col_wait(place_of, send, recv, chunks):
        order = [(c, k) for c in range(chunks) for k in reversed(range(chips - 1))]
        to_partner = {"col": partner}
        for c, k in order:
            there = chip_at(k)
            block = place_of(there * 2 + core, c)
            remote(block, send(there, c), recv(there, c), to_partner).wait_recv()
            remote(block, send(chips + there, c), recv(chips + there, c), to_partner).start()
        for c in range(chunks):
            remote(place_of(partner, c), send(chip, c), recv(chip, c), to_partner).wait_recv()
        for c, k in order:
            there = chip_at(k)
            block = place_of(there * 2 + 1 - core, c)
            remote(block, send(chips + there, c), recv(chips + there, c), to_partner).wait_recv()
        for c, k in order:
            there = chip_at(k)
            remote(place_of(col, c), send(there, c), recv(chip, c), to_partner).wait_send()
            block = place_of(there * 2 + core, c)
            remote(block, send(chips + there, c), recv(chips + there, c), to_partner).wait_send()
        for c in range(chunks):
            remote(place_of(col, c), send(chip, c), recv(chip, c), to_partner).wait_send()

    def whole(buffer, send, recv):
        return (lambda i, c: buffer.at[i], lambda k, c: send.at[k], lambda k, c: recv.at[k])

    def sliced(buffer, send, recv, now):
        size = slots // CHUNKS
        return (
            lambda i, c: buffer.at[now, i, c * size : (c + 1) * size],
            lambda k, c: send.at[now, k, c],
            lambda k, c: recv.at[now, k, c],
        )

    xi = whole(x_init, xi_send, xi_recv)
    ci = whole(c_init, ci_send, ci_recv)
    yi = whole(y_init, yi_send, yi_recv)
    local[0].wait()
    pl.semaphore_wait(barrier, (n_row - 1) + (chips - 1) + 1)
    row_send(*xi, 0)
    for copy in local[1:3]:
        copy.wait()
    col_send(*yi, 0)
    for copy in local[3:6]:
        copy.wait()
    row_send(*ci, 0)

    def pair_up(q, carry):
        for half in range(2):
            tile = tiles[2 * q + half]
            for out, data in ((plain, tile), (flipped, tile.T)):
                high = data.astype(jnp.bfloat16)
                out[q, 0:128, half * 128 : half * 128 + 128] = high
                out[q, 128:256, half * 128 : half * 128 + 128] = (
                    data - high.astype(jnp.float32)
                ).astype(jnp.bfloat16)
        return carry

    for i in range(TILE_PARTS):
        tile_copies[i].wait()
        lax.fori_loop(i * part // 2, (i + 1) * part // 2, pair_up, 0, unroll=2)

    def column_of(init, i, at):
        return init[i, at : at + SUB, :].T[:slots, 0:1]

    def own_ids(init, me, at):
        ids = column_of(init, me, at)
        return jnp.where(ids < 0.0, -2.0, ids)

    def hot_of(ids, first, share, column, hot, init, at, n):
        for i in range(n):
            column[i * slots : (i + 1) * slots, :] = jnp.broadcast_to(column_of(init, i, at), (slots, 128))
        wide = column[...].T[0:1, :]
        own = first + lax.broadcasted_iota(jnp.int32, (share, 1), 0)
        hot[0:slots, :] = jnp.where(ids == wide, 1.0, 0.0).astype(jnp.bfloat16)
        hot[slots : slots + share, :] = jnp.where(own.astype(jnp.float32) == wide, 1.0, 0.0).astype(jnp.bfloat16)

    def pick_of(ids, blocks):
        lanes = lax.broadcasted_iota(jnp.int32, (slots, blocks), 1).astype(jnp.float32)
        return jnp.where(ids == lanes, 1.0, 0.0).astype(jnp.bfloat16)

    def place_state(state, pick, init, at, share, me, n):
        state[0:slots, :] = split_dot(pick, init[:, at : at + share, :].reshape(n * share, 128))
        state[slots : slots + share, :] = init[me, at : at + share, :]

    def products(pairs, vectors, out, send):
        line = lax.broadcasted_iota(jnp.int32, (SUB, 128), 0)
        per_chunk = slots // SUB // CHUNKS

        def group(g, carry):
            at = pl.multiple_of(g * SUB, SUB)
            left = jnp.concatenate(pieces_of(vectors[pl.ds(at, SUB), :]), axis=0).astype(jnp.bfloat16)
            left = jnp.concatenate([left, left], axis=1)
            result = jnp.zeros((SUB, 128), jnp.float32)
            for q in range(SUB // 2):
                both = jnp.dot(left, pairs[g * (SUB // 2) + q], preferred_element_type=jnp.float32)
                total = (both[2 * SUB :] + both[SUB : 2 * SUB]) + both[:SUB]
                result = jnp.where(line == 2 * q, total[:, :128], result)
                result = jnp.where(line == 2 * q + 1, total[:, 128:], result)
            out[pl.ds(at, SUB), :] = result
            return carry

        for c in range(CHUNKS):
            lax.fori_loop(c * per_chunk, (c + 1) * per_chunk, group, 0, unroll=UNROLL)
            send(c)

    def forward(now):
        z = sliced(z_all, z_send, z_recv, now)
        products(flipped, extrapolated, z_all.at[now, col], lambda c: col_send(*z, c))

    row_wait(*xi, 1)
    col_ids = own_ids(x_init, row, sx)
    x_pick = pick_of(col_ids, n_row * sx)
    place_state(x_state, x_pick, x_init, 0, sx, row, n_row)
    extrapolated[...] = x_state[0:slots, :]
    forward(0)

    hot_of(col_ids, row * sx, sx, x_column, x_hot, x_init, sx, n_row)
    row_wait(*ci, 1)
    place_state(c_state, x_pick, c_init, 0, sx, row, n_row)
    place_state(l_state, x_pick, c_init, sx, sx, row, n_row)
    place_state(u_state, x_pick, c_init, 2 * sx, sx, row, n_row)
    col_wait(*yi, 1)
    row_ids = own_ids(y_init, col, 2 * sy)
    y_pick = pick_of(row_ids, n_col * sy)
    place_state(y_state, y_pick, y_init, 0, sy, col, n_col)
    place_state(b_state, y_pick, y_init, sy, sy, col, n_col)
    hot_of(row_ids, col * sy, sy, y_column, y_hot, y_init, 2 * sy, n_col)
    y_total[...] = jnp.zeros_like(y_total)
    x_total[...] = jnp.zeros_like(x_total)

    def iteration(step, carry):
        now = step % 2
        z = sliced(z_all, z_send, z_recv, now)
        p = sliced(p_all, p_send, p_recv, now)
        col_wait(*z, CHUNKS)
        applied = split_dot(y_hot[...], z_all[now].reshape(n_col * slots, 128))
        y_new = jnp.maximum(y_state[...] + dual_step * (b_state[...] - applied), 0.0)
        y_state[...] = y_new
        products(plain, y_state, p_all.at[now, row], lambda c: row_send(*p, c))
        y_total[...] += y_new[slots:, :]
        row_wait(*p, CHUNKS)
        transposed = split_dot(x_hot[...], p_all[now].reshape(n_row * slots, 128))
        x_old = x_state[...]
        moved = x_old - primal_step * (c_state[...] - transposed)
        x_new = jnp.minimum(jnp.maximum(moved, l_state[...]), u_state[...])
        x_state[...] = x_new
        extrapolated[...] = 2.0 * x_new[:slots, :] - x_old[:slots, :]

        @pl.when(step < ITERS - 1)
        def _():
            forward(1 - now)

        x_total[...] += x_new[slots:, :]
        return carry

    lax.fori_loop(0, ITERS, iteration, 0)

    primal_last[...] = x_state[slots:, :]
    dual_last[...] = y_state[slots:, :]
    primal_mean[...] = x_total[...] / ITERS
    dual_mean[...] = y_total[...] / ITERS


def body(n_row, n_col, tiles, tile_row, tile_col, tile_count, cost, rhs, lower, upper, primal_start, dual_start):
    slots, bs = tiles.shape[0], tiles.shape[2]
    blocks = [a.reshape(-1, bs) for a in (cost, rhs, lower, upper, primal_start, dual_start)]
    sx, sy = blocks[0].shape[0], blocks[1].shape[0]
    f32 = jnp.float32
    chips = n_col // 2
    vmem = pl.BlockSpec(memory_space=pltpu.VMEM)
    hbm = pl.BlockSpec(memory_space=pltpu.HBM)
    dma = pltpu.SemaphoreType.DMA
    state = lambda share: pltpu.VMEM((slots + share, bs), f32)
    out = pl.pallas_call(
        functools.partial(kernel, n_row, n_col),
        out_shape=[jax.ShapeDtypeStruct((s, bs), f32) for s in (sx, sy, sx, sy)],
        in_specs=[hbm] * 10,
        out_specs=[vmem] * 4,
        scratch_shapes=[
            pltpu.VMEM(tiles.shape, f32),
            pltpu.VMEM((slots // 2, 2 * bs, 2 * bs), jnp.bfloat16),
            pltpu.VMEM((slots // 2, 2 * bs, 2 * bs), jnp.bfloat16),
            pltpu.VMEM((n_col, 2 * sy + SUB, bs), f32),
            pltpu.VMEM((n_row, sx + SUB, bs), f32),
            pltpu.VMEM((n_row, 3 * sx, bs), f32),
            pltpu.VMEM((2, n_col, slots, bs), f32),
            pltpu.VMEM((2, n_row, slots, bs), f32),
            pltpu.VMEM((slots + sy, n_col * slots), jnp.bfloat16),
            pltpu.VMEM((slots + sx, n_row * slots), jnp.bfloat16),
            pltpu.VMEM((n_col * slots, bs), f32),
            pltpu.VMEM((n_row * slots, bs), f32),
            state(sy), state(sy), state(sx), state(sx), state(sx), state(sx),
            pltpu.VMEM((slots, bs), f32),
            pltpu.VMEM((sy, bs), f32),
            pltpu.VMEM((sx, bs), f32),
            pltpu.VMEM((1, slots), jnp.int32), pltpu.VMEM((1, slots), jnp.int32), pltpu.VMEM((1, 1), jnp.int32),
            dma((TILE_PARTS,)), dma((9,)),
            dma((2, 2 * chips, CHUNKS)), dma((2, 2 * chips, CHUNKS)),
            dma((2, n_row, CHUNKS)), dma((2, n_row, CHUNKS)),
            dma((2 * chips,)), dma((2 * chips,)),
            dma((n_row,)), dma((n_row,)),
            dma((n_row,)), dma((n_row,)),
        ],
        compiler_params=pltpu.CompilerParams(
            collective_id=0, has_side_effects=True, vmem_limit_bytes=VMEM_BYTES
        ),
        name="pdhg",
    )(tiles, tile_row.reshape(1, slots), tile_col.reshape(1, slots), tile_count, *blocks)
    return tuple(a.reshape(1, -1) for a in out)


def solution(mesh):
    return jax.shard_map(
        functools.partial(body, mesh.shape["row"], mesh.shape["col"]),
        mesh=mesh,
        in_specs=(
            P("row", "col", None),
            P("row", "col"),
            P("row", "col"),
            P("row", "col"),
            P("col", "row"),
            P("row", "col"),
            P("col", "row"),
            P("col", "row"),
            P("col", "row"),
            P("row", "col"),
        ),
        out_specs=(P("col", "row"), P("row", "col"), P("col", "row"), P("row", "col")),
        check_vma=False,
    )
```
